1024 devices in a mesh: gx: 8 (over y), gy: 4 (over x_hi), gz: 32 (over z, x_lo, core).
Axes of the slice: x: 8 (x_hi: 4, x_lo: 2; x = x_hi * 2 + x_lo), y: 8, z: 8, core: 2. Of those that a mesh axis runs over, the one named last changes fastest.
Arguments:
- trial: bfloat16 [16, 8, 128, 64, 128], P('gx', 'gy', 'gz'), may hold values from -6 to 6
- onsite: bfloat16 [16, 8, 128, 128, 128], P('gx', 'gy', 'gz'), as said below
- coupling: bfloat16 [3, 16, 8, 128, 128, 128], P(None, 'gx', 'gy', 'gz'), may hold values from -0.1875 to 0.1875
- bonds: int32 [3, 16, 8, 128], P(None, 'gx', 'gy', 'gz'), may hold values 0 or 1
Outputs:
- filtered: float32 [16, 8, 128, 64, 128], P('gx', 'gy', 'gz')
The draws below stay inside these ranges and needn't reach their ends.
Inputs may be any that keep to these rules, and one draw needn't show every extreme that they name: `onsite`: each on-site block is symmetric in its last two dimensions.
All inputs are finite; a program needn't handle non-finite values. No bound on the sum of `bonds` on one device may be relied on, other than what follows from the above.
Results may differ from the reference program's by a relative error of at most 0.0052.
Values may be sent and summed in bfloat16 or wider, within the bound.
No kernel may reach another device: no remote copies, remote signals or barrier semaphores. Data moves between devices by JAX's collectives and lax.ppermute only.
A program may use at most 32 MiB of HBM per device.

```python
import jax
import jax.numpy as jnp
from jax import lax

ORB = 128
VEC = 64
STEPS = 5
NX = 16
NY = 8
NZ = 128


def draw_onsite(key, part):
    sigma = (7.0 * ORB) ** (-0.5)
    raw = jax.random.normal(key, (NX, NY, NZ, ORB, ORB), jnp.float32)
    sym = (raw + jnp.swapaxes(raw, -1, -2)) * (sigma * 0.70710678)
    return sym.astype(jnp.bfloat16)


def plant(entries, key, low, high):
    longest = entries.shape.index(max(entries.shape))
    spots = []
    for shift in (0, 1):
        where = [jax.random.randint(jax.random.fold_in(key, axis), (), 0, length) for axis, length in enumerate(entries.shape)]
        where[longest] = (where[longest] + shift) % entries.shape[longest]
        spots.append(tuple(where))
    return entries.at[spots[0]].set(low).at[spots[1]].set(high)


def block_levels(stream_key, dims, split, least, top_value):
    def one(position, shards_of):
        steps = jax.random.uniform(jax.random.fold_in(jax.random.fold_in(stream_key, 6), position), (shards_of,), jnp.float32, least / len(split), top_value / len(split))
        return jnp.repeat(jnp.exp(steps), dims[position] // shards_of).reshape((-1,) + (1,) * (len(dims) - position - 1))

    level = one(*split[0])
    for cut in split[1:]:
        level = level * one(*cut)
    return level


def normal_values(stream_key, extent, scale, most, split=(), held_as=jnp.bfloat16):
    result = jax.random.normal(stream_key, extent, jnp.float32) * scale
    if len(split) > 0:
        result = block_levels(stream_key, extent, split, -0.22, 0.18) * result
    return jnp.clip(result, min=-most, max=most).astype(held_as)


def setup_inputs(seed: int = 0) -> dict:
    keys = jax.random.split(jax.random.key(seed), 5)
    return {
        "trial": normal_values(keys[0], (NX, NY, NZ, VEC, ORB), 1.0, 6.0, ((0, 8), (1, 4), (2, 32))),
        "onsite": draw_onsite(jax.random.fold_in(keys[4], 71), 0),
        "coupling": normal_values(keys[2], (3, NX, NY, NZ, ORB, ORB), (7 * ORB) ** -0.5, 0.1875, ((1, 8), (2, 4), (3, 32))),
        "bonds": plant((jax.random.randint(keys[3], (3, NX, NY, NZ), 0, 8) < 7).astype(jnp.int32), jax.random.fold_in(keys[3], 1), 0, 1),
    }


center_shift = 0.25
half_inverse = 0.5


def block_apply(blocks, vecs):
    return jnp.einsum("...pq,...kq->...kp", blocks.astype(jnp.float32), vecs.astype(jnp.float32))


def block_transposed(blocks, vecs):
    return jnp.einsum("...pq,...kp->...kq", blocks.astype(jnp.float32), vecs.astype(jnp.float32))


def apply_hamiltonian(vecs, onsite, coupling, masks):
    padded = jnp.pad(vecs, ((1, 1), (1, 1), (1, 1), (0, 0), (0, 0)))

    def one_slice(index):
        here = lax.dynamic_index_in_dim(vecs, index, 0, keepdims=False)
        after = lax.dynamic_index_in_dim(padded, index + 2, 0, keepdims=False)[1:-1, 1:-1]
        before = lax.dynamic_index_in_dim(padded, index, 0, keepdims=False)[1:-1, 1:-1]
        local_site = lax.dynamic_index_in_dim(onsite, index, 0, keepdims=False)
        blocks = lax.dynamic_index_in_dim(coupling, index, 1, keepdims=False)
        mask_here = lax.dynamic_index_in_dim(masks, index, 1, keepdims=False)
        below = jnp.maximum(index - 1, 0).astype(jnp.int32)
        prev_blocks = lax.dynamic_index_in_dim(coupling, below, 1, keepdims=False)
        prev_mask = lax.dynamic_index_in_dim(masks, below, 1, keepdims=False)[0] * (index > 0).astype(jnp.float32)
        total = block_apply(local_site, here)
        total = total + block_apply(blocks[0], after) * mask_here[0][..., None, None]
        total = total + block_transposed(prev_blocks[0], before) * prev_mask[..., None, None]
        upper_y = jnp.concatenate([here[1:], jnp.zeros_like(here[:1])], axis=0)
        total = total + block_apply(blocks[1], upper_y) * mask_here[1][..., None, None]
        term_y = block_transposed(blocks[1], here) * mask_here[1][..., None, None]
        total = total + jnp.concatenate([jnp.zeros_like(term_y[:1]), term_y[:-1]], axis=0)
        upper_z = jnp.concatenate([here[:, 1:], jnp.zeros_like(here[:, :1])], axis=1)
        total = total + block_apply(blocks[2], upper_z) * mask_here[2][..., None, None]
        term_z = block_transposed(blocks[2], here) * mask_here[2][..., None, None]
        total = total + jnp.concatenate([jnp.zeros_like(term_z[:, :1]), term_z[:, :-1]], axis=1)
        return total

    return lax.map(one_slice, jnp.arange(vecs.shape[0], dtype=jnp.int32))


def reference(trial, onsite, coupling, bonds):
    masks = bonds.astype(jnp.float32)

    def scaled(vecs):
        image = apply_hamiltonian(vecs, onsite, coupling, masks)
        return half_inverse * (image - center_shift * vecs.astype(jnp.float32))

    previous = trial
    current = scaled(trial).astype(jnp.bfloat16)
    for step in range(STEPS - 2):
        following = (2.0 * scaled(current) - previous.astype(jnp.float32)).astype(jnp.bfloat16)
        previous = current
        current = following
    return 2.0 * scaled(current) - previous.astype(jnp.float32)
```

```python
import jax
import jax.numpy as jnp
from jax import lax
from jax.experimental import pallas as pl
from jax.experimental.pallas import tpu as pltpu
from jax.sharding import PartitionSpec as P


STEPS = 5
CENTER_SHIFT = 0.25
HALF_INVERSE = 0.5

F32 = jnp.float32
BF16 = jnp.bfloat16
AXES = ("gx", "gy", "gz")


def places(lengths):
    nx, ny, nz = lengths
    return [(x, y, z) for x in range(nx) for y in range(ny) for z in range(nz)]


def number(place, lengths):
    return (place[0] * lengths[1] + place[1]) * lengths[2] + place[2]


def stepped(place, axis, by):
    moved = list(place)
    moved[axis] += by
    return tuple(moved)


def face(lengths, axis, layer):
    return [number(p, lengths) for p in places(lengths) if p[axis] == layer]


def plain(vecs, blocks):
    left = vecs[0] if len(vecs) == 1 else jnp.concatenate(vecs, axis=1)
    right = blocks[0] if len(blocks) == 1 else jnp.concatenate(blocks, axis=0)
    return lax.dot_general(left, right, (((1,), (0,)), ((), ())), preferred_element_type=F32)


def crossed(vecs, blocks):
    left = vecs[0] if len(vecs) == 1 else jnp.concatenate(vecs, axis=1)
    right = blocks[0] if len(blocks) == 1 else jnp.concatenate(blocks, axis=1)
    return lax.dot_general(left, right, (((1,), (1,)), ((), ())), preferred_element_type=F32)


def is_even_on(axis):
    return lax.rem(lax.axis_index(AXES[axis]), 2) == 0


def write_messages(lengths, vecs, blocks, sends):
    for axis in range(3):
        low = face(lengths, axis, 0)
        top = face(lengths, axis, lengths[axis] - 1)
        first, second = sends[2 * axis], sends[2 * axis + 1]
        is_even = is_even_on(axis)
        for i in range(len(top)):
            term = plain([vecs[top[i]]], [blocks[axis, top[i]]])
            below = vecs[low[i]].astype(F32)
            first[i] = jnp.where(is_even, term, below).astype(BF16)
            second[i] = jnp.where(is_even, below, term).astype(BF16)


def prepare(lengths, bonds, trial, coupling, blocks, *sends):
    for axis in range(3):
        for p in places(lengths):
            c = number(p, lengths)
            blocks[axis, c] = coupling[axis, c] * bonds[axis, p[0], p[1], p[2]].astype(F32).astype(BF16)
    write_messages(lengths, trial, blocks, sends)


def interior(lengths, vecs, onsite, blocks, total):
    for p in places(lengths):
        c = number(p, lengths)
        vs, ms, ws, ns = [vecs[c]], [onsite[c]], [], []
        for axis in range(3):
            if p[axis] > 0:
                lower = number(stepped(p, axis, -1), lengths)
                vs.append(vecs[lower])
                ms.append(blocks[axis, lower])
            if p[axis] < lengths[axis] - 1:
                upper = number(stepped(p, axis, 1), lengths)
                ws.append(vecs[upper])
                ns.append(blocks[axis, c])
        inside = plain(vs, ms)
        total[c] = inside + crossed(ws, ns) if ws else inside


def finish(lengths, step, total, vecs, previous, blocks, *refs):
    got, result, sends = refs[:6], refs[6], refs[7:]
    evens = [is_even_on(axis) for axis in range(3)]
    for p in places(lengths):
        c = number(p, lengths)
        value = total[c]
        ws, ns = [], []
        for axis in range(3):
            is_even = evens[axis]
            first, second = got[2 * axis], got[2 * axis + 1]
            if p[axis] == lengths[axis] - 1:
                i = face(lengths, axis, p[axis]).index(c)
                ws.append(jnp.where(is_even, first[i], second[i]))
                ns.append(blocks[axis, c])
            if p[axis] == 0:
                i = face(lengths, axis, 0).index(c)
                value = value + jnp.where(is_even, second[i], first[i]).astype(F32)
        if ws:
            value = value + crossed(ws, ns)
        shifted = value - CENTER_SHIFT * vecs[c].astype(F32)
        if step == 0:
            following = HALF_INVERSE * shifted
        else:
            following = 2.0 * HALF_INVERSE * shifted - previous[c].astype(F32)
        result[c] = following.astype(result.dtype)
    if sends:
        write_messages(lengths, result, blocks, sends)


def call(body, operands, scalars, shapes, flops):
    in_specs = [pl.BlockSpec(memory_space=pltpu.SMEM)] * len(scalars)
    in_specs += [pl.BlockSpec(memory_space=pltpu.VMEM)] * len(operands)
    moved = sum(a.size * a.dtype.itemsize for a in operands) + sum(s.size * s.dtype.itemsize for s in shapes)
    return pl.pallas_call(
        body,
        out_shape=shapes,
        in_specs=in_specs,
        out_specs=[pl.BlockSpec(memory_space=pltpu.VMEM)] * len(shapes),
        cost_estimate=pl.CostEstimate(flops=flops, bytes_accessed=moved, transcendentals=0),
        compiler_params=pltpu.CompilerParams(vmem_limit_bytes=24 << 20),
    )(*scalars, *operands)


def routes(axis):
    n = lax.axis_size(axis)
    pairs = [(i, i + 1) for i in range(0, n - 1, 2)]
    others = [(i, i + 1) for i in range(1, n - 1, 2)]
    both = lambda links: links + [(j, i) for i, j in links]
    return both(pairs), both(others)


def exchanged(sends):
    got = []
    for axis in range(3):
        for which, route in enumerate(routes(AXES[axis])):
            got.append(lax.ppermute(sends[2 * axis + which], AXES[axis], route))
    return got


def shards(trial, onsite, coupling, bonds):
    lengths = trial.shape[:3]
    k, q = trial.shape[3:]
    cells = lengths[0] * lengths[1] * lengths[2]
    vecs = trial.reshape(cells, k, q)
    onsite = onsite.reshape(cells, q, q)
    coupling = coupling.reshape(3, cells, q, q)
    message_shapes = []
    for axis in range(3):
        message_shapes += [jax.ShapeDtypeStruct((cells // lengths[axis], k, q), BF16)] * 2
    one = 2 * k * q * q
    faces = sum(cells // n for n in lengths)
    blocks, *sends = call(
        lambda *r: prepare(lengths, *r),
        [vecs, coupling],
        [bonds],
        [jax.ShapeDtypeStruct(coupling.shape, BF16)] + message_shapes,
        faces * one,
    )
    previous = vecs
    for step in range(STEPS):
        last = step == STEPS - 1
        got = exchanged(sends)
        (total,) = call(
            lambda *r: interior(lengths, *r),
            [vecs, onsite, blocks],
            [],
            [jax.ShapeDtypeStruct((cells, k, q), F32)],
            (7 * cells - 2 * faces) * one,
        )
        result = jax.ShapeDtypeStruct((cells, k, q), F32 if last else BF16)
        following, *sends = call(
            lambda *r, step=step: finish(lengths, step, *r),
            [total, vecs, previous, blocks, *got],
            [],
            [result] if last else [result] + message_shapes,
            (faces if last else 2 * faces) * one,
        )
        previous, vecs = vecs, following
    return vecs.reshape(trial.shape)


def solution(mesh):
    placed = (
        P("gx", "gy", "gz", None, None),
        P("gx", "gy", "gz", None, None),
        P(None, "gx", "gy", "gz", None, None),
        P(None, "gx", "gy", "gz"),
    )
    return jax.shard_map(
        shards,
        mesh=mesh,
        in_specs=placed,
        out_specs=P("gx", "gy", "gz", None, None),
        check_vma=False,
    )
```

```python
import jax
import jax.numpy as jnp
from jax import lax
from jax.experimental import pallas as pl
from jax.experimental.pallas import tpu as pltpu
from jax.sharding import PartitionSpec as P


STEPS = 5
CENTER_SHIFT = 0.25
HALF_INVERSE = 0.5

F32 = jnp.float32
BF16 = jnp.bfloat16
AXES = ("gx", "gy", "gz")


def places(lengths):
    nx, ny, nz = lengths
    return [(x, y, z) for x in range(nx) for y in range(ny) for z in range(nz)]


def number(place, lengths):
    return (place[0] * lengths[1] + place[1]) * lengths[2] + place[2]


def stepped(place, axis, by):
    moved = list(place)
    moved[axis] += by
    return tuple(moved)


def face(lengths, axis, layer):
    return [number(p, lengths) for p in places(lengths) if p[axis] == layer]


def plain(vecs, blocks):
    left = vecs[0] if len(vecs) == 1 else jnp.concatenate(vecs, axis=1)
    right = blocks[0] if len(blocks) == 1 else jnp.concatenate(blocks, axis=0)
    return lax.dot_general(left, right, (((1,), (0,)), ((), ())), preferred_element_type=F32)


def crossed(vecs, blocks):
    left = vecs[0] if len(vecs) == 1 else jnp.concatenate(vecs, axis=1)
    right = blocks[0] if len(blocks) == 1 else jnp.concatenate(blocks, axis=1)
    return lax.dot_general(left, right, (((1,), (1,)), ((), ())), preferred_element_type=F32)


def is_even_on(axis):
    return lax.rem(lax.axis_index(AXES[axis]), 2) == 0


def write_messages(lengths, vecs, blocks, sends, axes=(0, 1, 2)):
    for axis in axes:
        low = face(lengths, axis, 0)
        top = face(lengths, axis, lengths[axis] - 1)
        first, second = sends[2 * axis], sends[2 * axis + 1]
        is_even = is_even_on(axis)
        for i in range(len(top)):
            term = plain([vecs[top[i]]], [blocks[axis, top[i]]])
            below = vecs[low[i]].astype(F32)
            first[i] = jnp.where(is_even, term, below).astype(BF16)
            second[i] = jnp.where(is_even, below, term).astype(BF16)


def prepare(lengths, bonds_in, trial_in, coupling_in, vecs, blocks, *refs):
    sends, bonds, vecs_done, bonds_done, blocks_done = refs[:6], refs[6], refs[7], refs[8], refs[9:]
    copies = [pltpu.make_async_copy(bonds_in, bonds, bonds_done)]
    copies.append(pltpu.make_async_copy(trial_in, vecs, vecs_done))
    copies += [pltpu.make_async_copy(coupling_in.at[a], blocks.at[a], blocks_done[a]) for a in range(3)]
    for copy in copies:
        copy.start()
    copies[0].wait()
    copies[1].wait()
    for axis in range(3):
        copies[2 + axis].wait()
        for p in places(lengths):
            c = number(p, lengths)
            blocks[axis, c] = blocks[axis, c] * bonds[axis, p[0], p[1], p[2]].astype(F32).astype(BF16)
        write_messages(lengths, vecs, blocks, sends, (axis,))


def interior(lengths, first_core, vecs, onsite, blocks, *totals):
    total = totals[-1]

    @pl.when(is_even_on(2) == first_core)
    def _():
        interior_sums(lengths, vecs, onsite, blocks, total)


def interior_sums(lengths, vecs, onsite, blocks, total):
    for p in places(lengths):
        c = number(p, lengths)
        vs, ms, ws, ns = [vecs[c]], [onsite[c]], [], []
        for axis in range(3):
            if p[axis] > 0:
                lower = number(stepped(p, axis, -1), lengths)
                vs.append(vecs[lower])
                ms.append(blocks[axis, lower])
            if p[axis] < lengths[axis] - 1:
                upper = number(stepped(p, axis, 1), lengths)
                ws.append(vecs[upper])
                ns.append(blocks[axis, c])
        inside = plain(vs, ms)
        total[c] = inside + crossed(ws, ns) if ws else inside


def finish(lengths, step, total, vecs, previous, blocks, *refs):
    got, result, sends, done = refs[:6], refs[6], refs[7:], None
    if step == STEPS - 1:
        target, result, done, sends = refs[6], refs[7], refs[8], ()
    evens = [is_even_on(axis) for axis in range(3)]
    copies = []
    for p in places(lengths):
        c = number(p, lengths)
        value = total[c]
        ws, ns = [], []
        for axis in range(3):
            is_even = evens[axis]
            first, second = got[2 * axis], got[2 * axis + 1]
            from_above, from_below = (first.at[1], first.at[0]) if axis == 2 else (first, first)
            if p[axis] == lengths[axis] - 1:
                i = face(lengths, axis, p[axis]).index(c)
                ws.append(jnp.where(is_even, from_above[i], second[i]))
                ns.append(blocks[axis, c])
            if p[axis] == 0:
                i = face(lengths, axis, 0).index(c)
                value = value + jnp.where(is_even, second[i], from_below[i]).astype(F32)
        if ws:
            value = value + crossed(ws, ns)
        shifted = value - CENTER_SHIFT * vecs[c].astype(F32)
        if step == 0:
            following = HALF_INVERSE * shifted
        else:
            following = 2.0 * HALF_INVERSE * shifted - previous[c].astype(F32)
        result[c] = following.astype(result.dtype)
        if done is not None and p[2] == lengths[2] - 1:
            run = pl.ds(c + 1 - lengths[2], lengths[2])
            copies.append(pltpu.make_async_copy(result.at[run], target.at[run], done.at[len(copies)]))
            copies[-1].start()
    if sends:
        write_messages(lengths, result, blocks, sends)
    for copy in copies:
        copy.wait()


def call(body, operands, shapes, flops, place=pltpu.VMEM, scratch=(), aliases={}):
    in_specs = [pl.BlockSpec(memory_space=pltpu.VMEM)] * len(operands)
    moved = sum(a.size * a.dtype.itemsize for a in operands) + sum(s.size * s.dtype.itemsize for s in shapes)
    return pl.pallas_call(
        body,
        out_shape=shapes,
        in_specs=in_specs,
        out_specs=[pl.BlockSpec(memory_space=place)] * len(shapes),
        scratch_shapes=scratch,
        input_output_aliases=aliases,
        cost_estimate=pl.CostEstimate(flops=flops, bytes_accessed=moved, transcendentals=0),
        compiler_params=pltpu.CompilerParams(vmem_limit_bytes=24 << 20),
    )(*operands)


def routes(axis):
    n = lax.axis_size(axis)
    pairs = [(i, i + 1) for i in range(0, n - 1, 2)]
    others = [(i, i + 1) for i in range(1, n - 1, 2)]
    both = lambda links: links + [(j, i) for i, j in links]
    return both(pairs), both(others)


def exchanged(sends):
    got = []
    for axis in range(3):
        for which, route in enumerate(routes(AXES[axis])):
            message = sends[2 * axis + which]
            if axis == 2 and which == 0:
                pairs = [[i, i + 1] for i in range(0, lax.axis_size(AXES[axis]), 2)]
                got.append(lax.all_gather(message, AXES[axis], axis_index_groups=pairs))
            else:
                got.append(lax.ppermute(message, AXES[axis], route))
    return got


def shards(trial, onsite, coupling, bonds):
    lengths = trial.shape[:3]
    k, q = trial.shape[3:]
    cells = lengths[0] * lengths[1] * lengths[2]
    vecs = trial.reshape(cells, k, q)
    onsite = onsite.reshape(cells, q, q)
    coupling = coupling.reshape(3, cells, q, q)
    message_shapes = []
    for axis in range(3):
        message_shapes += [jax.ShapeDtypeStruct((cells // lengths[axis], k, q), BF16)] * 2
    one = 2 * k * q * q
    ending = (pltpu.VMEM((cells, k, q), F32), pltpu.SemaphoreType.DMA((lengths[0] * lengths[1],)))
    faces = sum(cells // n for n in lengths)
    shapes = [jax.ShapeDtypeStruct(vecs.shape, BF16), jax.ShapeDtypeStruct(coupling.shape, BF16)] + message_shapes
    vecs, blocks, *sends = pl.pallas_call(
        lambda *r: prepare(lengths, *r),
        out_shape=shapes,
        in_specs=[pl.BlockSpec(memory_space=pltpu.HBM)] * 3,
        out_specs=[pl.BlockSpec(memory_space=pltpu.VMEM)] * len(shapes),
        scratch_shapes=[pltpu.SMEM(bonds.shape, jnp.int32)] + [pltpu.SemaphoreType.DMA] * 5,
        cost_estimate=pl.CostEstimate(flops=faces * one, bytes_accessed=4 << 20, transcendentals=0),
        compiler_params=pltpu.CompilerParams(vmem_limit_bytes=24 << 20),
        name="prepare",
    )(*[pltpu.with_memory_space_constraint(a, pltpu.HBM) for a in (bonds, vecs, coupling)])
    previous = vecs
    for step in range(STEPS):
        last = step == STEPS - 1
        got = exchanged(sends)
        sums, inside = [jax.ShapeDtypeStruct((cells, k, q), F32)], (7 * cells - 2 * faces) * one
        total = call(lambda *r: interior(lengths, False, *r), [vecs, onsite, blocks], sums, inside)
        (total,) = call(
            lambda *r: interior(lengths, True, *r), [vecs, onsite, blocks, *total], sums, inside, aliases={3: 0}
        )
        result = jax.ShapeDtypeStruct((cells, k, q), F32 if last else BF16)
        following, *sends = call(
            lambda *r, step=step: finish(lengths, step, *r),
            [total, vecs, previous, blocks, *got],
            [result] if last else [result] + message_shapes,
            (faces if last else 2 * faces) * one,
            *((pltpu.HBM, ending) if last else ()),
        )
        previous, vecs = vecs, following
    return vecs.reshape(trial.shape)


def solution(mesh):
    placed = (
        P("gx", "gy", "gz", None, None),
        P("gx", "gy", "gz", None, None),
        P(None, "gx", "gy", "gz", None, None),
        P(None, "gx", "gy", "gz"),
    )
    return jax.shard_map(
        shards,
        mesh=mesh,
        in_specs=placed,
        out_specs=P("gx", "gy", "gz", None, None),
        check_vma=False,
    )
```

```python
import jax
import jax.numpy as jnp
from jax import lax
from jax.experimental import pallas as pl
from jax.experimental.pallas import tpu as pltpu
from jax.sharding import PartitionSpec as P


STEPS = 5
CENTER_SHIFT = 0.25
HALF_INVERSE = 0.5

F32 = jnp.float32
BF16 = jnp.bfloat16
AXES = ("gx", "gy", "gz")


def places(lengths):
    nx, ny, nz = lengths
    return [(x, y, z) for x in range(nx) for y in range(ny) for z in range(nz)]


def number(place, lengths):
    return (place[0] * lengths[1] + place[1]) * lengths[2] + place[2]


def stepped(place, axis, by):
    moved = list(place)
    moved[axis] += by
    return tuple(moved)


def face(lengths, axis, layer):
    return [number(p, lengths) for p in places(lengths) if p[axis] == layer]


def plain(vecs, blocks):
    left = vecs[0] if len(vecs) == 1 else jnp.concatenate(vecs, axis=1)
    right = blocks[0] if len(blocks) == 1 else jnp.concatenate(blocks, axis=0)
    return lax.dot_general(left, right, (((1,), (0,)), ((), ())), preferred_element_type=F32)


def crossed(vecs, blocks):
    left = vecs[0] if len(vecs) == 1 else jnp.concatenate(vecs, axis=1)
    right = blocks[0] if len(blocks) == 1 else jnp.concatenate(blocks, axis=1)
    return lax.dot_general(left, right, (((1,), (1,)), ((), ())), preferred_element_type=F32)


def is_even_on(axis):
    return lax.rem(lax.axis_index(AXES[axis]), 2) == 0


def write_messages(lengths, vecs, blocks, sends, axes=(0, 1, 2)):
    for axis in axes:
        low = face(lengths, axis, 0)
        top = face(lengths, axis, lengths[axis] - 1)
        first, second = sends[2 * axis], sends[2 * axis + 1]
        is_even = is_even_on(axis)
        for i in range(len(top)):
            term = plain([vecs[top[i]]], [blocks[axis, top[i]]])
            below = vecs[low[i]].astype(F32)
            first[i] = jnp.where(is_even, term, below).astype(BF16)
            second[i] = jnp.where(is_even, below, term).astype(BF16)


def prepare(lengths, bonds_in, trial_in, coupling_in, vecs, blocks, *refs):
    sends, bonds, vecs_done, bonds_done, blocks_done = refs[:6], refs[6], refs[7], refs[8], refs[9:]
    copies = [pltpu.make_async_copy(bonds_in, bonds, bonds_done)]
    copies.append(pltpu.make_async_copy(trial_in, vecs, vecs_done))
    copies += [pltpu.make_async_copy(coupling_in.at[a], blocks.at[a], blocks_done[a]) for a in range(3)]
    for copy in copies:
        copy.start()
    copies[0].wait()
    copies[1].wait()
    for axis in range(3):
        copies[2 + axis].wait()
        for p in places(lengths):
            c = number(p, lengths)
            blocks[axis, c] = blocks[axis, c] * bonds[axis, p[0], p[1], p[2]].astype(F32).astype(BF16)
        write_messages(lengths, vecs, blocks, sends, (axis,))


def interior(lengths, vecs, onsite, blocks, total):
    for p in places(lengths):
        c = number(p, lengths)
        vs, ms, ws, ns = [vecs[c]], [onsite[c]], [], []
        for axis in range(3):
            if p[axis] > 0:
                lower = number(stepped(p, axis, -1), lengths)
                vs.append(vecs[lower])
                ms.append(blocks[axis, lower])
            if p[axis] < lengths[axis] - 1:
                upper = number(stepped(p, axis, 1), lengths)
                ws.append(vecs[upper])
                ns.append(blocks[axis, c])
        inside = plain(vs, ms)
        total[c] = inside + crossed(ws, ns) if ws else inside


def finish(lengths, step, total, vecs, previous, blocks, *refs):
    got, result, sends, done = refs[:6], refs[6], refs[7:], None
    if step == STEPS - 1:
        target, result, done, sends = refs[6], refs[7], refs[8], ()
    evens = [is_even_on(axis) for axis in range(3)]
    copies = []
    for p in places(lengths):
        c = number(p, lengths)
        value = total[c]
        ws, ns = [], []
        for axis in range(3):
            is_even = evens[axis]
            first, second = got[2 * axis], got[2 * axis + 1]
            from_above, from_below = (first.at[1], first.at[0]) if axis == 2 else (first, first)
            if p[axis] == lengths[axis] - 1:
                i = face(lengths, axis, p[axis]).index(c)
                ws.append(jnp.where(is_even, from_above[i], second[i]))
                ns.append(blocks[axis, c])
            if p[axis] == 0:
                i = face(lengths, axis, 0).index(c)
                value = value + jnp.where(is_even, second[i], from_below[i]).astype(F32)
        if ws:
            value = value + crossed(ws, ns)
        shifted = value - CENTER_SHIFT * vecs[c].astype(F32)
        if step == 0:
            following = HALF_INVERSE * shifted
        else:
            following = 2.0 * HALF_INVERSE * shifted - previous[c].astype(F32)
        result[c] = following.astype(result.dtype)
        if done is not None and p[2] == lengths[2] - 1:
            run = pl.ds(c + 1 - lengths[2], lengths[2])
            copies.append(pltpu.make_async_copy(result.at[run], target.at[run], done.at[len(copies)]))
            copies[-1].start()
    if sends:
        write_messages(lengths, result, blocks, sends)
    for copy in copies:
        copy.wait()


def call(body, operands, shapes, flops, place=pltpu.VMEM, scratch=()):
    in_specs = [pl.BlockSpec(memory_space=pltpu.VMEM)] * len(operands)
    moved = sum(a.size * a.dtype.itemsize for a in operands) + sum(s.size * s.dtype.itemsize for s in shapes)
    return pl.pallas_call(
        body,
        out_shape=shapes,
        in_specs=in_specs,
        out_specs=[pl.BlockSpec(memory_space=place)] * len(shapes),
        scratch_shapes=scratch,
        cost_estimate=pl.CostEstimate(flops=flops, bytes_accessed=moved, transcendentals=0),
        compiler_params=pltpu.CompilerParams(vmem_limit_bytes=24 << 20),
    )(*operands)


def routes(axis):
    n = lax.axis_size(axis)
    pairs = [(i, i + 1) for i in range(0, n - 1, 2)]
    others = [(i, i + 1) for i in range(1, n - 1, 2)]
    both = lambda links: links + [(j, i) for i, j in links]
    return both(pairs), both(others)


def exchanged(sends):
    got = []
    for axis in range(3):
        for which, route in enumerate(routes(AXES[axis])):
            message = sends[2 * axis + which]
            if axis == 2 and which == 0:
                pairs = [[i, i + 1] for i in range(0, lax.axis_size(AXES[axis]), 2)]
                got.append(lax.all_gather(message, AXES[axis], axis_index_groups=pairs))
            else:
                got.append(lax.ppermute(message, AXES[axis], route))
    return got


def shards(trial, onsite, coupling, bonds):
    lengths = trial.shape[:3]
    k, q = trial.shape[3:]
    cells = lengths[0] * lengths[1] * lengths[2]
    vecs = trial.reshape(cells, k, q)
    onsite = onsite.reshape(cells, q, q)
    coupling = coupling.reshape(3, cells, q, q)
    message_shapes = []
    for axis in range(3):
        message_shapes += [jax.ShapeDtypeStruct((cells // lengths[axis], k, q), BF16)] * 2
    one = 2 * k * q * q
    ending = (pltpu.VMEM((cells, k, q), F32), pltpu.SemaphoreType.DMA((lengths[0] * lengths[1],)))
    faces = sum(cells // n for n in lengths)
    shapes = [jax.ShapeDtypeStruct(vecs.shape, BF16), jax.ShapeDtypeStruct(coupling.shape, BF16)] + message_shapes
    vecs, blocks, *sends = pl.pallas_call(
        lambda *r: prepare(lengths, *r),
        out_shape=shapes,
        in_specs=[pl.BlockSpec(memory_space=pltpu.HBM)] * 3,
        out_specs=[pl.BlockSpec(memory_space=pltpu.VMEM)] * len(shapes),
        scratch_shapes=[pltpu.SMEM(bonds.shape, jnp.int32)] + [pltpu.SemaphoreType.DMA] * 5,
        cost_estimate=pl.CostEstimate(flops=faces * one, bytes_accessed=4 << 20, transcendentals=0),
        compiler_params=pltpu.CompilerParams(vmem_limit_bytes=24 << 20),
        name="prepare",
    )(*[pltpu.with_memory_space_constraint(a, pltpu.HBM) for a in (bonds, vecs, coupling)])
    previous = vecs
    for step in range(STEPS):
        last = step == STEPS - 1
        got = exchanged(sends)
        (total,) = call(
            lambda *r: interior(lengths, *r),
            [vecs, onsite, blocks],
            [jax.ShapeDtypeStruct((cells, k, q), F32)],
            (7 * cells - 2 * faces) * one,
        )
        result = jax.ShapeDtypeStruct((cells, k, q), F32 if last else BF16)
        following, *sends = call(
            lambda *r, step=step: finish(lengths, step, *r),
            [total, vecs, previous, blocks, *got],
            [result] if last else [result] + message_shapes,
            (faces if last else 2 * faces) * one,
            *((pltpu.HBM, ending) if last else ()),
        )
        previous, vecs = vecs, following
    return vecs.reshape(trial.shape)


def solution(mesh):
    placed = (
        P("gx", "gy", "gz", None, None),
        P("gx", "gy", "gz", None, None),
        P(None, "gx", "gy", "gz", None, None),
        P(None, "gx", "gy", "gz"),
    )
    return jax.shard_map(
        shards,
        mesh=mesh,
        in_specs=placed,
        out_specs=P("gx", "gy", "gz", None, None),
        check_vma=False,
    )
```
